32 devices in a mesh: dp: 4 (over y, core), vocab: 8 (over z, x).
Axes of the slice: x: 2, y: 2, z: 4, core: 2. Of those that a mesh axis runs over, the one named last changes fastest.
Arguments:
- hidden_rows: bfloat16 [640, 8192], P('dp'), may hold values from -6 to 6
- translator: bfloat16 [8192, 8192], P(None, 'vocab'), may hold values from -0.0625 to 0.0625
- final_gain: float32 [8192], replicated, may hold values from 0.5 to 1.5
- unembed: bfloat16 [8192, 16384], P('dp', 'vocab'), may hold values from -8 to 8
- target_logits: bfloat16 [640, 16384], P('dp', 'vocab'), may hold values from -40 to 300
Outputs:
- grad_translator: float32 [8192, 8192], P('dp', 'vocab')
- row_kl: float32 [640], P('dp')
The draws below stay inside these ranges and needn't reach their ends.
All inputs are finite; a program needn't handle non-finite values.
Results may differ from the reference program's by a relative error of at most 0.0077.
Values may be sent and summed in bfloat16 or wider, within the bound.
A program may use at most 128 MiB of HBM per device.

```python
import math
import jax
import jax.numpy as jnp
from jax import lax

D = 8192
V = 16384
ROWS = 640


def draw_unembed(key, part):
    keys = jax.random.split(key, 2)
    col_scale = jnp.exp(jax.random.uniform(keys[1], (V,), minval=0.0, maxval=math.log(10.0)))
    base = jax.random.normal(keys[0], (D, V))
    weights = base * col_scale[None, :] * (0.06 / math.sqrt(D))
    return jnp.clip(weights, -8.0, 8.0).astype(jnp.bfloat16)


def draw_target_logits(key, part):
    keys = jax.random.split(key, 2)
    row_scale = jnp.exp(jax.random.uniform(keys[1], (ROWS, 1), minval=0.0, maxval=math.log(10.0)))
    values = jax.random.uniform(keys[0], (ROWS, V), minval=-3.464, maxval=3.464) * row_scale
    return jnp.clip(values, -40.0, 300.0).astype(jnp.bfloat16)


def spiked(drawn, stream_key, source, target, blocks, factor):
    owner, partner = [(jnp.arange(drawn.shape[position]) // (drawn.shape[position] // blocks)).reshape([-1 if axis == position else 1 for axis in range(drawn.ndim)]) for position in (source, target)]
    chosen = jax.random.permutation(stream_key, blocks)[partner]
    strong = (owner == chosen) | (owner == (partner + blocks // 2) % blocks)
    return jnp.where(strong, factor * drawn, drawn)


def levels(stream_key, extent, cuts, smallest, top_value):
    factor_of = 1.0
    for dim, parts in cuts:
        draws = jax.random.uniform(jax.random.fold_in(jax.random.fold_in(stream_key, 6), dim), (parts,), jnp.float32, smallest / len(cuts), top_value / len(cuts))
        factor_of = factor_of * jnp.repeat(jnp.exp(draws), extent[dim] // parts).reshape((-1,) + (1,) * (len(extent) - 1 - dim))
    return factor_of


def gaussian(rng, dims, spread, most, cuts=(), held_as=jnp.bfloat16):
    entries = spread * jax.random.normal(rng, dims, jnp.float32)
    if cuts:
        entries = entries * levels(rng, dims, cuts, -0.22, 0.18)
    return jnp.clip(entries, -most, most).astype(held_as)


def bell_draw_with(rng, shape, scale, reach, cuts, heavy, held_as=jnp.bfloat16):
    entries = scale * jax.random.normal(rng, shape, jnp.float32)
    if cuts:
        entries = entries * levels(rng, shape, cuts, -0.22, 0.18)
    return jnp.clip(spiked(entries, jax.random.fold_in(rng, 3), *heavy), -reach, reach).astype(held_as)


def setup_inputs(seed: int = 0) -> dict:
    splits = jax.random.split(jax.random.key(seed), 6)
    hidden_rows = bell_draw_with(splits[0], (ROWS, D), 1.0, 6.0, ((0, 4),), (0, 1, 4, 2.0))
    translator = gaussian(splits[1], (D, D), D ** -0.5, 0.0625, ((1, 8),))
    final_gain = jnp.clip(1.0 + 0.1 * jax.random.normal(splits[2], (D,), jnp.float32), 0.5, 1.5)
    unembed = draw_unembed(jax.random.fold_in(splits[5], 71), 0)
    target_logits = draw_target_logits(jax.random.fold_in(splits[5], 71), 0)
    return {"hidden_rows": hidden_rows, "translator": translator, "final_gain": final_gain, "unembed": unembed, "target_logits": target_logits}


EPSILON = 1e-05

def reference(hidden_rows, translator, final_gain, unembed, target_logits):
    translated = (hidden_rows.astype(jnp.float32) + jnp.dot(hidden_rows, translator, preferred_element_type=jnp.float32)).astype(jnp.bfloat16)
    trans_values = translated.astype(jnp.float32)
    inv_rms = lax.rsqrt(lax.optimization_barrier(jnp.mean(trans_values * trans_values, axis=1, keepdims=True)) + EPSILON)
    normed = (trans_values * inv_rms * final_gain).astype(jnp.bfloat16)
    logits = jnp.dot(normed, unembed, preferred_element_type=jnp.float32)
    target = target_logits.astype(jnp.float32)
    log_model = jax.nn.log_softmax(logits, axis=1)
    log_target = jax.nn.log_softmax(target, axis=1)
    prob_target = jnp.exp(log_target)
    row_kl = lax.optimization_barrier(jnp.sum(prob_target * (log_target - log_model), axis=1))
    grad_logits = (jnp.exp(log_model) - prob_target).astype(jnp.bfloat16)
    grad_normed = lax.dot_general(grad_logits, unembed, (((1,), (1,)), ((), ())), preferred_element_type=jnp.float32)
    scaled = grad_normed * final_gain
    inner = lax.optimization_barrier(jnp.mean(trans_values * scaled, axis=1, keepdims=True))
    grad_translated = (inv_rms * scaled - trans_values * inv_rms ** 3 * inner).astype(jnp.bfloat16)
    grad_translator = lax.dot_general(hidden_rows, grad_translated, (((0,), (0,)), ((), ())), preferred_element_type=jnp.float32)
    return (grad_translator, row_kl)
```

```python
import functools

import jax
import jax.numpy as jnp
from jax import lax
from jax.experimental import pallas as pl
from jax.experimental.pallas import tpu as pltpu
from jax.sharding import PartitionSpec as P

EPSILON = 1e-05
LOGIT_SCALE = 0.5
GRAD_SCALE = 2048.0
MESH = pl.DeviceIdType.MESH


def greet(barrier, targets):
    total = jnp.int32(0)
    for wanted, device in targets:
        @pl.when(wanted)
        def _():
            pl.semaphore_signal(barrier, inc=1, device_id=device, device_id_type=MESH)

        total = total + jnp.where(wanted, 1, 0)
    pl.semaphore_wait(barrier, total)


def gather_kernel(axis, count, src, out, send_sem, recv_sem, own_sem):
    pos = {"dp": lax.axis_index("dp"), "vocab": lax.axis_index("vocab")}
    me = pos[axis]

    def at(step):
        other = dict(pos)
        other[axis] = lax.rem(me + step, count)
        return other["dp"], other["vocab"]

    barrier = pltpu.get_barrier_semaphore()
    for step in range(1, count):
        pl.semaphore_signal(barrier, inc=1, device_id=at(step), device_id_type=MESH)
    own = pltpu.make_async_copy(src, out.at[me], own_sem)
    own.start()
    pl.semaphore_wait(barrier, count - 1)

    def copy(step, slot):
        return pltpu.make_async_remote_copy(
            src_ref=src, dst_ref=out.at[slot], send_sem=send_sem.at[step],
            recv_sem=recv_sem.at[slot], device_id=at(step), device_id_type=MESH,
        )

    for step in range(1, count):
        copy(step, me).start()
    own.wait()
    for step in range(1, count):
        copy(step, lax.rem(me + count - step, count)).wait_recv()
    for step in range(1, count):
        copy(step, me).wait_send()


def small_gather(values, axis, count, cid):
    return pl.pallas_call(
        functools.partial(gather_kernel, axis, count),
        out_shape=jax.ShapeDtypeStruct((count,) + values.shape, values.dtype),
        in_specs=[pl.BlockSpec(memory_space=pltpu.VMEM)],
        out_specs=pl.BlockSpec(memory_space=pltpu.VMEM),
        scratch_shapes=[
            pltpu.SemaphoreType.DMA((count,)),
            pltpu.SemaphoreType.DMA((count,)),
            pltpu.SemaphoreType.DMA,
        ],
        compiler_params=pltpu.CompilerParams(collective_id=cid, has_side_effects=True),
    )(values)


def slice_kernel(dp, per, src, out, chain, right_sem, left_sem, hop_sem, send_sem, recv_sem, own_sem):
    rows, cols = src.shape
    d, v = lax.axis_index("dp"), lax.axis_index("vocab")
    q, r = lax.div(v, per), lax.rem(v, per)
    barrier = pltpu.get_barrier_semaphore()
    group = [
        (jnp.logical_or(d != i, r != j), (i, q * per + j)) for i in range(dp) for j in range(per)
    ]
    right, left = (d, lax.rem(v + per, dp * per)), (d, lax.rem(v + (dp - 1) * per, dp * per))
    greet(barrier, group + [(q < dp - 1, right), (q > 0, left)])

    def hop(block, ref, device, sem):
        return pltpu.make_async_remote_copy(
            src_ref=ref, dst_ref=chain.at[block], send_sem=sem.at[block],
            recv_sem=hop_sem.at[block], device_id=device, device_id_type=MESH,
        )

    def place(i, j):
        return out.at[pl.ds(pl.multiple_of(i * rows, 16), rows), pl.ds(pl.multiple_of(j * cols, 128), cols)]

    def deliver(block, ref, j):
        return pltpu.make_async_remote_copy(
            src_ref=ref, dst_ref=place(d, r), send_sem=send_sem.at[block * per + j],
            recv_sem=recv_sem.at[d * per + r], device_id=(block, q * per + j), device_id_type=MESH,
        )

    def send_out(block, ref):
        for step in range(per):
            j = lax.rem(r + step, per)
            mine = jnp.logical_and(block == d, j == r)

            @pl.when(jnp.logical_not(mine))
            def _():
                deliver(block, ref, j).start()

            @pl.when(mine)
            def _():
                pltpu.make_async_copy(ref, place(d, r), own_sem).start()

    @pl.when(q < dp - 1)
    def _():
        hop(q, src, right, right_sem).start()

    @pl.when(q > 0)
    def _():
        hop(q, src, left, left_sem).start()

    send_out(q, src)
    for k in range(1, dp):
        for block, valid, more, device, sem in (
            (q - k, q - k >= 0, q < dp - 1, right, right_sem),
            (q + k, q + k < dp, q > 0, left, left_sem),
        ):
            @pl.when(valid)
            def _():
                hop(block, src, device, sem).wait_recv()

                @pl.when(more)
                def _():
                    hop(block, chain.at[block], device, sem).start()

                send_out(block, chain.at[block])

    for i in range(dp):
        for j in range(per):
            mine = jnp.logical_and(d == i, r == j)

            @pl.when(mine)
            def _():
                pltpu.make_async_copy(src, place(i, j), own_sem).wait()

            @pl.when(jnp.logical_not(mine))
            def _():
                pltpu.make_async_remote_copy(
                    src_ref=src, dst_ref=place(i, j), send_sem=send_sem.at[i * per + j],
                    recv_sem=recv_sem.at[i * per + j], device_id=(i, q * per + j), device_id_type=MESH,
                ).wait()

    for block in range(dp):
        @pl.when(jnp.logical_and(block <= q, q < dp - 1))
        def _():
            hop(block, src, right, right_sem).wait_send()

        @pl.when(jnp.logical_and(block >= q, q > 0))
        def _():
            hop(block, src, left, left_sem).wait_send()


def feature_slices(own_part, dp, vocab):
    rows, cols = own_part.shape
    per = vocab // dp
    dma = pltpu.SemaphoreType.DMA
    return pl.pallas_call(
        functools.partial(slice_kernel, dp, per),
        out_shape=jax.ShapeDtypeStruct((dp * rows, per * cols), own_part.dtype),
        in_specs=[pl.BlockSpec(memory_space=pltpu.VMEM)],
        out_specs=pl.BlockSpec(memory_space=pltpu.VMEM),
        scratch_shapes=[
            pltpu.VMEM((dp, rows, cols), own_part.dtype),
            dma((dp,)), dma((dp,)), dma((dp,)), dma((vocab,)), dma((vocab,)), dma,
        ],
        compiler_params=pltpu.CompilerParams(collective_id=1, has_side_effects=True),
    )(own_part)


def return_parts(values, dp, vocab):
    per = vocab // dp
    rows, cols = values.shape[0] // dp, values.shape[1] // per
    v = lax.axis_index("vocab")
    q, r = v // per, v % per
    total = None
    for i in range(dp):
        for j in range(per):
            block = lax.dynamic_slice(
                values, ((q + i) % dp * rows, (r + j) % per * cols), (rows, cols)
            )
            pairs = [
                (d * vocab + a * per + b, (a + i) % dp * vocab + d * per + (b + j) % per)
                for d in range(dp) for a in range(dp) for b in range(per)
            ]
            got = lax.ppermute((block * GRAD_SCALE).astype(jnp.float16), ("dp", "vocab"), pairs).astype(jnp.float32)
            total = got if total is None else total + got
    return total * (1.0 / GRAD_SCALE)


def local(dp, vocab, hidden_rows, translator, final_gain, unembed, target_logits):
    row_count, feature_count = hidden_rows.shape
    col_count = translator.shape[1]
    slice_count = unembed.shape[0]
    dp_index, vocab_index = lax.axis_index("dp"), lax.axis_index("vocab")
    first_col = vocab_index * col_count
    own_inputs = lax.dynamic_slice_in_dim(hidden_rows, first_col, col_count, 1).astype(jnp.float32)
    own_part = (
        own_inputs + jnp.dot(hidden_rows, translator, preferred_element_type=jnp.float32)
    ).astype(jnp.bfloat16)
    value_cols = own_part.astype(jnp.float32)
    translated = feature_slices(own_part, dp, vocab).astype(jnp.float32)
    squares = small_gather(jnp.sum(translated * translated, axis=1).reshape(dp, row_count), "dp", dp, 3)
    all_rms = lax.rsqrt(jnp.sum(squares, axis=0) / feature_count + EPSILON)
    inv_rms = lax.dynamic_slice_in_dim(all_rms, dp_index, 1, 0).reshape(row_count, 1)
    gain_slice = lax.dynamic_slice_in_dim(final_gain, dp_index * slice_count, slice_count, 0)
    normed_slices = (translated * all_rms.reshape(-1, 1) * gain_slice).astype(jnp.bfloat16)
    logit_parts = lax.all_to_all(
        (jnp.dot(normed_slices, unembed, preferred_element_type=jnp.float32) * LOGIT_SCALE)
        .astype(jnp.float16)
        .reshape(dp, row_count, -1),
        "dp",
        split_axis=0,
        concat_axis=0,
    )
    logits = jnp.sum(logit_parts.astype(jnp.float32), axis=0) * (1.0 / LOGIT_SCALE)
    target = target_logits.astype(jnp.float32)
    own_top = jnp.max(logits, axis=1)
    own_target_top = jnp.max(target, axis=1)
    model_exp = jnp.exp(logits - own_top[:, None])
    target_exp = jnp.exp(target - own_target_top[:, None])
    stats = small_gather(
        jnp.stack(
            [
                own_top,
                own_target_top,
                jnp.sum(model_exp, axis=1),
                jnp.sum(target_exp, axis=1),
                jnp.sum(target_exp * (target - logits), axis=1),
            ]
        ),
        "vocab",
        vocab,
        5,
    )
    model_top = jnp.max(stats[:, 0], axis=0)
    target_top = jnp.max(stats[:, 1], axis=0)
    model_total = jnp.sum(stats[:, 2] * jnp.exp(stats[:, 0] - model_top), axis=0)
    target_weight = jnp.exp(stats[:, 1] - target_top)
    target_total = jnp.sum(stats[:, 3] * target_weight, axis=0)
    cross_total = jnp.sum(stats[:, 4] * target_weight, axis=0)
    row_kl = (
        cross_total / target_total
        - (target_top + jnp.log(target_total))
        + (model_top + jnp.log(model_total))
    )
    prob_model = jnp.exp(logits - model_top[:, None]) / model_total[:, None]
    prob_target = jnp.exp(target - target_top[:, None]) / target_total[:, None]
    grad_logits = (prob_model - prob_target).astype(jnp.bfloat16)
    back_slices = lax.dot_general(
        lax.all_gather(grad_logits, "dp", axis=0, tiled=True),
        unembed,
        (((1,), (1,)), ((), ())),
        preferred_element_type=jnp.float32,
    )
    input_slices = lax.all_to_all(hidden_rows, "dp", split_axis=1, concat_axis=0, tiled=True)
    grad_cols = return_parts(back_slices, dp, vocab)
    gain_cols = lax.dynamic_slice_in_dim(final_gain, first_col, col_count, 0)
    scaled = grad_cols * gain_cols
    inner_parts = small_gather(jnp.sum(value_cols * scaled, axis=1)[None], "vocab", vocab, 6)
    inner = jnp.sum(inner_parts, axis=0).reshape(row_count, 1) / feature_count
    grad_translated = (inv_rms * scaled - value_cols * inv_rms**3 * inner).astype(jnp.bfloat16)
    grad_translator = lax.dot_general(
        input_slices,
        lax.all_gather(grad_translated, "dp", axis=0, tiled=True),
        (((0,), (0,)), ((), ())),
        preferred_element_type=jnp.float32,
    )
    return (grad_translator, row_kl)


def solution(mesh):
    return jax.shard_map(
        functools.partial(local, mesh.shape["dp"], mesh.shape["vocab"]),
        mesh=mesh,
        in_specs=(P("dp", None), P(None, "vocab"), P(), P("dp", "vocab"), P("dp", "vocab")),
        out_specs=(P("dp", "vocab"), P("dp")),
        check_vma=False,
    )
```

```python
import functools

import jax
import jax.numpy as jnp
from jax import lax
from jax.experimental import pallas as pl
from jax.experimental.pallas import tpu as pltpu
from jax.sharding import PartitionSpec as P

EPSILON = 1e-05
LOGIT_SCALE = 0.5
GRAD_SCALE = 2048.0
MESH = pl.DeviceIdType.MESH


def greet(barrier, targets):
    total = jnp.int32(0)
    for wanted, device in targets:
        @pl.when(wanted)
        def _():
            pl.semaphore_signal(barrier, inc=1, device_id=device, device_id_type=MESH)

        total = total + jnp.where(wanted, 1, 0)
    pl.semaphore_wait(barrier, total)


def gather_kernel(axis, count, src, out, send_sem, recv_sem, own_sem):
    pos = {"dp": lax.axis_index("dp"), "vocab": lax.axis_index("vocab")}
    me = pos[axis]

    def at(step):
        other = dict(pos)
        other[axis] = lax.rem(me + step, count)
        return other["dp"], other["vocab"]

    barrier = pltpu.get_barrier_semaphore()
    for step in range(1, count):
        pl.semaphore_signal(barrier, inc=1, device_id=at(step), device_id_type=MESH)
    own = pltpu.make_async_copy(src, out.at[me], own_sem)
    own.start()
    pl.semaphore_wait(barrier, count - 1)

    def copy(step, slot):
        return pltpu.make_async_remote_copy(
            src_ref=src, dst_ref=out.at[slot], send_sem=send_sem.at[step],
            recv_sem=recv_sem.at[slot], device_id=at(step), device_id_type=MESH,
        )

    for step in range(1, count):
        copy(step, me).start()
    own.wait()
    for step in range(1, count):
        copy(step, lax.rem(me + count - step, count)).wait_recv()
    for step in range(1, count):
        copy(step, me).wait_send()


def small_gather(values, axis, count, cid):
    return pl.pallas_call(
        functools.partial(gather_kernel, axis, count),
        out_shape=jax.ShapeDtypeStruct((count,) + values.shape, values.dtype),
        in_specs=[pl.BlockSpec(memory_space=pltpu.VMEM)],
        out_specs=pl.BlockSpec(memory_space=pltpu.VMEM),
        scratch_shapes=[
            pltpu.SemaphoreType.DMA((count,)),
            pltpu.SemaphoreType.DMA((count,)),
            pltpu.SemaphoreType.DMA,
        ],
        compiler_params=pltpu.CompilerParams(collective_id=cid, has_side_effects=True),
    )(values)


def rows_kernel(dp, src, out, far_send, near_send, recv_sem, own_sem):
    d, v = lax.axis_index("dp"), lax.axis_index("vocab")
    low = lax.rem(d, 2)
    mate = d + 1 - 2 * low
    barrier = pltpu.get_barrier_semaphore()
    for device in [mate] + [lax.rem(d + 2 * s, dp) for s in range(1, dp // 2)]:
        pl.semaphore_signal(barrier, inc=1, device_id=(device, v), device_id_type=MESH)
    own = pltpu.make_async_copy(src, out.at[0], own_sem)
    own.start()
    pl.semaphore_wait(barrier, dp // 2)

    def slot(step):
        return lax.rem(2 * step + 1 - 2 * low + dp, dp)

    def far(step):
        return pltpu.make_async_remote_copy(
            src_ref=src, dst_ref=out.at[2 * step], send_sem=far_send.at[step],
            recv_sem=recv_sem.at[2 * step], device_id=(lax.rem(d + 2 * step, dp), v), device_id_type=MESH,
        )

    def near(step):
        return pltpu.make_async_remote_copy(
            src_ref=src if step == 0 else out.at[2 * step], dst_ref=out.at[slot(step)],
            send_sem=near_send.at[step], recv_sem=recv_sem.at[slot(step)],
            device_id=(mate, v), device_id_type=MESH,
        )

    for step in range(1, dp // 2):
        far(step).start()
    near(0).start()
    for step in range(1, dp // 2):
        far(step).wait_recv()
        near(step).start()
    own.wait()
    for step in range(dp // 2):
        pltpu.make_async_remote_copy(
            src_ref=src, dst_ref=out.at[2 * step + 1], send_sem=near_send.at[step],
            recv_sem=recv_sem.at[2 * step + 1], device_id=(mate, v), device_id_type=MESH,
        ).wait_recv()
    for step in range(1, dp // 2):
        far(step).wait_send()
    for step in range(dp // 2):
        near(step).wait_send()


def gather_rows(values, dp, cid):
    dma = pltpu.SemaphoreType.DMA
    return pl.pallas_call(
        functools.partial(rows_kernel, dp),
        out_shape=jax.ShapeDtypeStruct((dp,) + values.shape, values.dtype),
        in_specs=[pl.BlockSpec(memory_space=pltpu.VMEM)],
        out_specs=pl.BlockSpec(memory_space=pltpu.VMEM),
        scratch_shapes=[dma((dp,)), dma((dp,)), dma((dp,)), dma],
        compiler_params=pltpu.CompilerParams(collective_id=cid, has_side_effects=True),
    )(values)


def slice_kernel(dp, per, src, out, chain, right_sem, left_sem, hop_sem, send_sem, recv_sem, own_sem):
    rows, cols = src.shape
    d, v = lax.axis_index("dp"), lax.axis_index("vocab")
    q, r = lax.div(v, per), lax.rem(v, per)
    barrier = pltpu.get_barrier_semaphore()
    group = [
        (jnp.logical_or(d != i, r != j), (i, q * per + j)) for i in range(dp) for j in range(per)
    ]
    right, left = (d, lax.rem(v + per, dp * per)), (d, lax.rem(v + (dp - 1) * per, dp * per))
    greet(barrier, group + [(q < dp - 1, right), (q > 0, left)])

    def hop(block, ref, device, sem):
        return pltpu.make_async_remote_copy(
            src_ref=ref, dst_ref=chain.at[block], send_sem=sem.at[block],
            recv_sem=hop_sem.at[block], device_id=device, device_id_type=MESH,
        )

    def place(i, j):
        return out.at[pl.ds(pl.multiple_of(i * rows, 16), rows), pl.ds(pl.multiple_of(j * cols, 128), cols)]

    def deliver(block, ref, j):
        return pltpu.make_async_remote_copy(
            src_ref=ref, dst_ref=place(d, r), send_sem=send_sem.at[block * per + j],
            recv_sem=recv_sem.at[d * per + r], device_id=(block, q * per + j), device_id_type=MESH,
        )

    def send_out(block, ref):
        for step in range(per):
            j = lax.rem(r + step, per)
            mine = jnp.logical_and(block == d, j == r)

            @pl.when(jnp.logical_not(mine))
            def _():
                deliver(block, ref, j).start()

            @pl.when(mine)
            def _():
                pltpu.make_async_copy(ref, place(d, r), own_sem).start()

    @pl.when(q < dp - 1)
    def _():
        hop(q, src, right, right_sem).start()

    @pl.when(q > 0)
    def _():
        hop(q, src, left, left_sem).start()

    send_out(q, src)
    for k in range(1, dp):
        for block, valid, more, device, sem in (
            (q - k, q - k >= 0, q < dp - 1, right, right_sem),
            (q + k, q + k < dp, q > 0, left, left_sem),
        ):
            @pl.when(valid)
            def _():
                hop(block, src, device, sem).wait_recv()

                @pl.when(more)
                def _():
                    hop(block, chain.at[block], device, sem).start()

                send_out(block, chain.at[block])

    for i in range(dp):
        for j in range(per):
            mine = jnp.logical_and(d == i, r == j)

            @pl.when(mine)
            def _():
                pltpu.make_async_copy(src, place(i, j), own_sem).wait()

            @pl.when(jnp.logical_not(mine))
            def _():
                pltpu.make_async_remote_copy(
                    src_ref=src, dst_ref=place(i, j), send_sem=send_sem.at[i * per + j],
                    recv_sem=recv_sem.at[i * per + j], device_id=(i, q * per + j), device_id_type=MESH,
                ).wait()

    for block in range(dp):
        @pl.when(jnp.logical_and(block <= q, q < dp - 1))
        def _():
            hop(block, src, right, right_sem).wait_send()

        @pl.when(jnp.logical_and(block >= q, q > 0))
        def _():
            hop(block, src, left, left_sem).wait_send()


def feature_slices(own_part, dp, vocab):
    rows, cols = own_part.shape
    per = vocab // dp
    dma = pltpu.SemaphoreType.DMA
    return pl.pallas_call(
        functools.partial(slice_kernel, dp, per),
        out_shape=jax.ShapeDtypeStruct((dp * rows, per * cols), own_part.dtype),
        in_specs=[pl.BlockSpec(memory_space=pltpu.VMEM)],
        out_specs=pl.BlockSpec(memory_space=pltpu.VMEM),
        scratch_shapes=[
            pltpu.VMEM((dp, rows, cols), own_part.dtype),
            dma((dp,)), dma((dp,)), dma((dp,)), dma((vocab,)), dma((vocab,)), dma,
        ],
        compiler_params=pltpu.CompilerParams(collective_id=1, has_side_effects=True),
    )(own_part)


def shifted(values, dp, per, by_d, by_q, by_r):
    vocab = dp * per
    pairs = [
        (d * vocab + q * per + r, (d + by_d) % dp * vocab + (q + by_q) % dp * per + (r + by_r) % per)
        for d in range(dp) for q in range(dp) for r in range(per)
    ]
    return lax.ppermute(values, ("dp", "vocab"), pairs)


def return_parts(values, dp, vocab, parts):
    per = vocab // dp
    v = lax.axis_index("vocab")
    d, q, r = lax.axis_index("dp"), v // per, v % per
    _, rows, width = values.shape
    cols = width // per // parts
    totals = []
    for part in range(parts):
        def columns(j):
            start = (r + j) % per * (width // per) + part * cols
            return lax.dynamic_slice(values, (0, 0, start), (dp, rows, cols)) * GRAD_SCALE

        summed = columns(0)
        for j in range(1, per):
            summed = summed + shifted(columns(j).astype(jnp.float16), dp, per, 0, 0, j).astype(jnp.float32)
        summed = summed.astype(jnp.float16)
        own = jnp.stack([summed[0]] + [shifted(summed[i], dp, per, -i, 0, 0) for i in range(1, dp)])
        total = lax.dynamic_index_in_dim(own, (q - d) % dp, 0, False).astype(jnp.float32)
        for k in range(1, dp):
            block = lax.dynamic_index_in_dim(own, (q + k - d) % dp, 0, False)
            total = total + shifted(block, dp, per, 0, k, 0).astype(jnp.float32)
        totals.append(total)
    return jnp.concatenate(totals, axis=1) * (1.0 / GRAD_SCALE)


def outer_kernel(*refs):
    *lefts, right, out = refs
    total = None
    for i, left in enumerate(lefts):
        term = lax.dot_general(
            left[...], right[i], (((0,), (0,)), ((), ())), preferred_element_type=jnp.float32
        )
        total = term if total is None else total + term
    out[...] = total


def row_outer(lefts, right):
    rows, features = lefts[0].shape
    cols = right.shape[2]
    tile = min(256, features)
    return pl.pallas_call(
        outer_kernel,
        grid=(features // tile,),
        out_shape=jax.ShapeDtypeStruct((features, cols), jnp.float32),
        in_specs=[pl.BlockSpec((rows, tile), lambda i: (0, i)) for _ in lefts]
        + [pl.BlockSpec(right.shape, lambda i: (0, 0, 0))],
        out_specs=pl.BlockSpec((tile, cols), lambda i: (i, 0)),
    )(*lefts, right)


def local(dp, vocab, hidden_rows, translator, final_gain, unembed, target_logits):
    row_count, feature_count = hidden_rows.shape
    col_count = translator.shape[1]
    slice_count = unembed.shape[0]
    dp_index, vocab_index = lax.axis_index("dp"), lax.axis_index("vocab")
    first_col = vocab_index * col_count
    own_inputs = lax.dynamic_slice_in_dim(hidden_rows, first_col, col_count, 1).astype(jnp.float32)
    own_part = (
        own_inputs + jnp.dot(hidden_rows, translator, preferred_element_type=jnp.float32)
    ).astype(jnp.bfloat16)
    value_cols = own_part.astype(jnp.float32)
    translated = feature_slices(own_part, dp, vocab).astype(jnp.float32)
    squares = small_gather(jnp.sum(translated * translated, axis=1).reshape(dp, row_count), "dp", dp, 3)
    all_rms = lax.rsqrt(jnp.sum(squares, axis=0) / feature_count + EPSILON)
    inv_rms = lax.dynamic_slice_in_dim(all_rms, dp_index, 1, 0).reshape(row_count, 1)
    gain_slice = lax.dynamic_slice_in_dim(final_gain, dp_index * slice_count, slice_count, 0)
    normed_slices = (translated * all_rms.reshape(-1, 1) * gain_slice).astype(jnp.bfloat16)
    logit_parts = lax.all_to_all(
        (jnp.dot(normed_slices, unembed, preferred_element_type=jnp.float32) * LOGIT_SCALE)
        .astype(jnp.float16)
        .reshape(dp, row_count, -1),
        "dp",
        split_axis=0,
        concat_axis=0,
    )
    logits = jnp.sum(logit_parts.astype(jnp.float32), axis=0) * (1.0 / LOGIT_SCALE)
    target = target_logits.astype(jnp.float32)
    own_top = jnp.max(logits, axis=1)
    own_target_top = jnp.max(target, axis=1)
    model_exp = jnp.exp(logits - own_top[:, None])
    target_exp = jnp.exp(target - own_target_top[:, None])
    stats = small_gather(
        jnp.stack(
            [
                own_top,
                own_target_top,
                jnp.sum(model_exp, axis=1),
                jnp.sum(target_exp, axis=1),
                jnp.sum(target_exp * (target - logits), axis=1),
            ]
        ),
        "vocab",
        vocab,
        5,
    )
    model_top = jnp.max(stats[:, 0], axis=0)
    target_top = jnp.max(stats[:, 1], axis=0)
    model_total = jnp.sum(stats[:, 2] * jnp.exp(stats[:, 0] - model_top), axis=0)
    target_weight = jnp.exp(stats[:, 1] - target_top)
    target_total = jnp.sum(stats[:, 3] * target_weight, axis=0)
    cross_total = jnp.sum(stats[:, 4] * target_weight, axis=0)
    row_kl = (
        cross_total / target_total
        - (target_top + jnp.log(target_total))
        + (model_top + jnp.log(model_total))
    )
    prob_model = jnp.exp(logits - model_top[:, None]) / model_total[:, None]
    prob_target = jnp.exp(target - target_top[:, None]) / target_total[:, None]
    grad_logits = (prob_model - prob_target).astype(jnp.bfloat16)
    all_grads, late_rows = lax.optimization_barrier((gather_rows(grad_logits, dp, 7), hidden_rows))
    back_slices = lax.dot_general(
        all_grads.reshape(dp * row_count, -1),
        unembed,
        (((1,), (1,)), ((), ())),
        preferred_element_type=jnp.float32,
    ).reshape(dp, row_count, slice_count)
    input_blocks = [
        shifted(
            lax.dynamic_slice_in_dim(late_rows, (dp_index + i) % dp * slice_count, slice_count, 1),
            dp, vocab // dp, i, 0, 0,
        )
        if i
        else lax.dynamic_slice_in_dim(late_rows, dp_index * slice_count, slice_count, 1)
        for i in range(dp)
    ]
    grad_cols = return_parts(back_slices, dp, vocab, 2)
    gain_cols = lax.dynamic_slice_in_dim(final_gain, first_col, col_count, 0)
    scaled = grad_cols * gain_cols
    inner_parts = small_gather(jnp.sum(value_cols * scaled, axis=1)[None], "vocab", vocab, 6)
    inner = jnp.sum(inner_parts, axis=0).reshape(row_count, 1) / feature_count
    grad_translated = (inv_rms * scaled - value_cols * inv_rms**3 * inner).astype(jnp.bfloat16)
    grad_translator = row_outer(input_blocks, gather_rows(grad_translated, dp, 8))
    return (grad_translator, row_kl)


def solution(mesh):
    return jax.shard_map(
        functools.partial(local, mesh.shape["dp"], mesh.shape["vocab"]),
        mesh=mesh,
        in_specs=(P("dp", None), P(None, "vocab"), P(), P("dp", "vocab"), P("dp", "vocab")),
        out_specs=(P("dp", "vocab"), P("dp")),
        check_vma=False,
    )
```

```python
import functools

import jax
import jax.numpy as jnp
from jax import lax
from jax.experimental import pallas as pl
from jax.experimental.pallas import tpu as pltpu
from jax.sharding import PartitionSpec as P


EPSILON = 1e-05
LOGIT_SCALE = 0.5
GRAD_SCALE = 2048.0
PARTS = 2
MESH = pl.DeviceIdType.MESH


def greet(barrier, targets):
    total = jnp.int32(0)
    for wanted, device in targets:
        @pl.when(wanted)
        def _():
            pl.semaphore_signal(barrier, inc=1, device_id=device, device_id_type=MESH)

        total = total + jnp.where(wanted, 1, 0)
    pl.semaphore_wait(barrier, total)


def gather_kernel(axis, count, src, out, send_sem, recv_sem, own_sem):
    pos = {"dp": lax.axis_index("dp"), "vocab": lax.axis_index("vocab")}
    me = pos[axis]

    def at(step):
        other = dict(pos)
        other[axis] = lax.rem(me + step, count)
        return other["dp"], other["vocab"]

    barrier = pltpu.get_barrier_semaphore()
    for step in range(1, count):
        pl.semaphore_signal(barrier, inc=1, device_id=at(step), device_id_type=MESH)
    own = pltpu.make_async_copy(src, out.at[me], own_sem)
    own.start()
    pl.semaphore_wait(barrier, count - 1)

    def copy(step, slot):
        return pltpu.make_async_remote_copy(
            src_ref=src, dst_ref=out.at[slot], send_sem=send_sem.at[step],
            recv_sem=recv_sem.at[slot], device_id=at(step), device_id_type=MESH,
        )

    for step in range(1, count):
        copy(step, me).start()
    own.wait()
    for step in range(1, count):
        copy(step, lax.rem(me + count - step, count)).wait_recv()
    for step in range(1, count):
        copy(step, me).wait_send()


def small_gather(values, axis, count, cid):
    return pl.pallas_call(
        functools.partial(gather_kernel, axis, count),
        out_shape=jax.ShapeDtypeStruct((count,) + values.shape, values.dtype),
        in_specs=[pl.BlockSpec(memory_space=pltpu.VMEM)],
        out_specs=pl.BlockSpec(memory_space=pltpu.VMEM),
        scratch_shapes=[
            pltpu.SemaphoreType.DMA((count,)),
            pltpu.SemaphoreType.DMA((count,)),
            pltpu.SemaphoreType.DMA,
        ],
        compiler_params=pltpu.CompilerParams(collective_id=cid, has_side_effects=True),
    )(values)


def rows_kernel(dp, src, out, far_send, near_send, recv_sem, own_sem):
    d, v = lax.axis_index("dp"), lax.axis_index("vocab")
    low = lax.rem(d, 2)
    mate = d + 1 - 2 * low
    barrier = pltpu.get_barrier_semaphore()
    for device in [mate] + [lax.rem(d + 2 * s, dp) for s in range(1, dp // 2)]:
        pl.semaphore_signal(barrier, inc=1, device_id=(device, v), device_id_type=MESH)
    own = pltpu.make_async_copy(src, out.at[0], own_sem)
    own.start()
    pl.semaphore_wait(barrier, dp // 2)

    def slot(step):
        return lax.rem(2 * step + 1 - 2 * low + dp, dp)

    def far(step):
        return pltpu.make_async_remote_copy(
            src_ref=src, dst_ref=out.at[2 * step], send_sem=far_send.at[step],
            recv_sem=recv_sem.at[2 * step], device_id=(lax.rem(d + 2 * step, dp), v), device_id_type=MESH,
        )

    def near(step):
        return pltpu.make_async_remote_copy(
            src_ref=src if step == 0 else out.at[2 * step], dst_ref=out.at[slot(step)],
            send_sem=near_send.at[step], recv_sem=recv_sem.at[slot(step)],
            device_id=(mate, v), device_id_type=MESH,
        )

    for step in range(1, dp // 2):
        far(step).start()
    near(0).start()
    for step in range(1, dp // 2):
        far(step).wait_recv()
        near(step).start()
    own.wait()
    for step in range(dp // 2):
        pltpu.make_async_remote_copy(
            src_ref=src, dst_ref=out.at[2 * step + 1], send_sem=near_send.at[step],
            recv_sem=recv_sem.at[2 * step + 1], device_id=(mate, v), device_id_type=MESH,
        ).wait_recv()
    for step in range(1, dp // 2):
        far(step).wait_send()
    for step in range(dp // 2):
        near(step).wait_send()


def gather_rows(values, dp, cid):
    dma = pltpu.SemaphoreType.DMA
    return pl.pallas_call(
        functools.partial(rows_kernel, dp),
        out_shape=jax.ShapeDtypeStruct((dp,) + values.shape, values.dtype),
        in_specs=[pl.BlockSpec(memory_space=pltpu.VMEM)],
        out_specs=pl.BlockSpec(memory_space=pltpu.VMEM),
        scratch_shapes=[dma((dp,)), dma((dp,)), dma((dp,)), dma],
        compiler_params=pltpu.CompilerParams(collective_id=cid, has_side_effects=True),
    )(values)


def slice_kernel(dp, per, src, out, chain, right_sem, left_sem, hop_sem, send_sem, recv_sem, own_sem):
    rows, cols = src.shape
    d, v = lax.axis_index("dp"), lax.axis_index("vocab")
    q, r = lax.div(v, per), lax.rem(v, per)
    barrier = pltpu.get_barrier_semaphore()
    group = [
        (jnp.logical_or(d != i, r != j), (i, q * per + j)) for i in range(dp) for j in range(per)
    ]
    right, left = (d, lax.rem(v + per, dp * per)), (d, lax.rem(v + (dp - 1) * per, dp * per))
    greet(barrier, group + [(q < dp - 1, right), (q > 0, left)])

    def hop(block, ref, device, sem):
        return pltpu.make_async_remote_copy(
            src_ref=ref, dst_ref=chain.at[block], send_sem=sem.at[block],
            recv_sem=hop_sem.at[block], device_id=device, device_id_type=MESH,
        )

    def place(i, j):
        return out.at[pl.ds(pl.multiple_of(i * rows, 16), rows), pl.ds(pl.multiple_of(j * cols, 128), cols)]

    def deliver(block, ref, j):
        return pltpu.make_async_remote_copy(
            src_ref=ref, dst_ref=place(d, r), send_sem=send_sem.at[block * per + j],
            recv_sem=recv_sem.at[d * per + r], device_id=(block, q * per + j), device_id_type=MESH,
        )

    def send_out(block, ref):
        for step in range(per):
            j = lax.rem(r + step, per)
            mine = jnp.logical_and(block == d, j == r)

            @pl.when(jnp.logical_not(mine))
            def _():
                deliver(block, ref, j).start()

            @pl.when(mine)
            def _():
                pltpu.make_async_copy(ref, place(d, r), own_sem).start()

    @pl.when(q < dp - 1)
    def _():
        hop(q, src, right, right_sem).start()

    @pl.when(q > 0)
    def _():
        hop(q, src, left, left_sem).start()

    send_out(q, src)
    for k in range(1, dp):
        for block, valid, more, device, sem in (
            (q - k, q - k >= 0, q < dp - 1, right, right_sem),
            (q + k, q + k < dp, q > 0, left, left_sem),
        ):
            @pl.when(valid)
            def _():
                hop(block, src, device, sem).wait_recv()

                @pl.when(more)
                def _():
                    hop(block, chain.at[block], device, sem).start()

                send_out(block, chain.at[block])

    for i in range(dp):
        for j in range(per):
            mine = jnp.logical_and(d == i, r == j)

            @pl.when(mine)
            def _():
                pltpu.make_async_copy(src, place(i, j), own_sem).wait()

            @pl.when(jnp.logical_not(mine))
            def _():
                pltpu.make_async_remote_copy(
                    src_ref=src, dst_ref=place(i, j), send_sem=send_sem.at[i * per + j],
                    recv_sem=recv_sem.at[i * per + j], device_id=(i, q * per + j), device_id_type=MESH,
                ).wait()

    for block in range(dp):
        @pl.when(jnp.logical_and(block <= q, q < dp - 1))
        def _():
            hop(block, src, right, right_sem).wait_send()

        @pl.when(jnp.logical_and(block >= q, q > 0))
        def _():
            hop(block, src, left, left_sem).wait_send()


def feature_slices(own_part, dp, vocab):
    rows, cols = own_part.shape
    per = vocab // dp
    dma = pltpu.SemaphoreType.DMA
    return pl.pallas_call(
        functools.partial(slice_kernel, dp, per),
        out_shape=jax.ShapeDtypeStruct((dp * rows, per * cols), own_part.dtype),
        in_specs=[pl.BlockSpec(memory_space=pltpu.VMEM)],
        out_specs=pl.BlockSpec(memory_space=pltpu.VMEM),
        scratch_shapes=[
            pltpu.VMEM((dp, rows, cols), own_part.dtype),
            dma((dp,)), dma((dp,)), dma((dp,)), dma((vocab,)), dma((vocab,)), dma,
        ],
        compiler_params=pltpu.CompilerParams(collective_id=1, has_side_effects=True),
    )(own_part)


def shifted(values, dp, per, by_d, by_q, by_r):
    vocab = dp * per
    pairs = [
        (d * vocab + q * per + r, (d + by_d) % dp * vocab + (q + by_q) % dp * per + (r + by_r) % per)
        for d in range(dp) for q in range(dp) for r in range(per)
    ]
    return lax.ppermute(values, ("dp", "vocab"), pairs)


def return_parts(products, dp, vocab):
    per = vocab // dp
    v = lax.axis_index("vocab")
    d, q, r = lax.axis_index("dp"), v // per, v % per
    totals = []
    for values in products:
        rows, cols = values.shape[1], values.shape[2] // per

        def columns(j):
            return lax.dynamic_slice(values, (0, 0, (r + j) % per * cols), (dp, rows, cols)) * GRAD_SCALE

        summed = columns(0)
        for j in range(1, per):
            summed = summed + shifted(columns(j).astype(jnp.float16), dp, per, 0, 0, j).astype(jnp.float32)
        summed = summed.astype(jnp.float16)
        own = jnp.stack([summed[0]] + [shifted(summed[i], dp, per, -i, 0, 0) for i in range(1, dp)])
        total = lax.dynamic_index_in_dim(own, (q - d) % dp, 0, False).astype(jnp.float32)
        for k in range(1, dp):
            block = lax.dynamic_index_in_dim(own, (q + k - d) % dp, 0, False)
            total = total + shifted(block, dp, per, 0, k, 0).astype(jnp.float32)
        totals.append(total)
    return jnp.concatenate(totals, axis=0) * (1.0 / GRAD_SCALE)


def outer_kernel(*refs):
    *lefts, right, out = refs
    total = None
    for i, left in enumerate(lefts):
        term = lax.dot_general(
            left[...], right[i], (((0,), (0,)), ((), ())), preferred_element_type=jnp.float32
        )
        total = term if total is None else total + term
    out[...] = total


def row_outer(lefts, right):
    rows, features = lefts[0].shape
    cols = right.shape[2]
    tile = min(256, features)
    return pl.pallas_call(
        outer_kernel,
        grid=(features // tile,),
        out_shape=jax.ShapeDtypeStruct((features, cols), jnp.float32),
        in_specs=[pl.BlockSpec((rows, tile), lambda i: (0, i)) for _ in lefts]
        + [pl.BlockSpec(right.shape, lambda i: (0, 0, 0))],
        out_specs=pl.BlockSpec((tile, cols), lambda i: (i, 0)),
    )(*lefts, right)


def local(dp, vocab, hidden_rows, translator, final_gain, unembed, target_logits):
    row_count, feature_count = hidden_rows.shape
    col_count = translator.shape[1]
    slice_count = unembed.shape[0]
    dp_index, vocab_index = lax.axis_index("dp"), lax.axis_index("vocab")
    first_col = vocab_index * col_count
    own_inputs = lax.dynamic_slice_in_dim(hidden_rows, first_col, col_count, 1).astype(jnp.float32)
    own_part = (
        own_inputs + jnp.dot(hidden_rows, translator, preferred_element_type=jnp.float32)
    ).astype(jnp.bfloat16)
    value_cols = own_part.astype(jnp.float32)
    per = vocab // dp

    def input_slice(i):
        return lax.dynamic_slice_in_dim(hidden_rows, (dp_index + i) % dp * slice_count, slice_count, 1)

    early = [i for i in range(1, dp) if i % 2 == 0]
    late = [i for i in range(1, dp) if i % 2]
    input_blocks = {0: input_slice(0)}
    delivered, early_blocks = lax.optimization_barrier(
        (feature_slices(own_part, dp, vocab), [input_slice(i) for i in early])
    )
    for i, block in zip(early, early_blocks):
        input_blocks[i] = shifted(block, dp, per, i, 0, 0)
    translated = delivered.astype(jnp.float32)
    squares = small_gather(jnp.sum(translated * translated, axis=1).reshape(dp, row_count), "dp", dp, 3)
    all_rms = lax.rsqrt(jnp.sum(squares, axis=0) / feature_count + EPSILON)
    inv_rms = lax.dynamic_slice_in_dim(all_rms, dp_index, 1, 0).reshape(row_count, 1)
    gain_slice = lax.dynamic_slice_in_dim(final_gain, dp_index * slice_count, slice_count, 0)
    normed_slices = (translated * all_rms.reshape(-1, 1) * gain_slice).astype(jnp.bfloat16)
    logit_sums = jnp.dot(normed_slices, unembed, preferred_element_type=jnp.float32) * LOGIT_SCALE
    logit_sums = logit_sums.astype(jnp.float16)
    logit_parts = lax.all_to_all(
        logit_sums.reshape(dp, row_count, -1),
        "dp",
        split_axis=0,
        concat_axis=0,
    )
    logits = jnp.sum(logit_parts.astype(jnp.float32), axis=0) * (1.0 / LOGIT_SCALE)
    target = target_logits.astype(jnp.float32)
    own_top = jnp.max(logits, axis=1)
    own_target_top = jnp.max(target, axis=1)
    model_exp = jnp.exp(logits - own_top[:, None])
    target_exp = jnp.exp(target - own_target_top[:, None])
    stats = small_gather(
        jnp.stack(
            [
                own_top,
                own_target_top,
                jnp.sum(model_exp, axis=1),
                jnp.sum(target_exp, axis=1),
                jnp.sum(target_exp * (target - logits), axis=1),
            ]
        ),
        "vocab",
        vocab,
        5,
    )
    model_top = jnp.max(stats[:, 0], axis=0)
    target_top = jnp.max(stats[:, 1], axis=0)
    model_total = jnp.sum(stats[:, 2] * jnp.exp(stats[:, 0] - model_top), axis=0)
    target_weight = jnp.exp(stats[:, 1] - target_top)
    target_total = jnp.sum(stats[:, 3] * target_weight, axis=0)
    cross_total = jnp.sum(stats[:, 4] * target_weight, axis=0)
    row_kl = (
        cross_total / target_total
        - (target_top + jnp.log(target_total))
        + (model_top + jnp.log(model_total))
    )
    prob_model = jnp.exp(logits - model_top[:, None]) / model_total[:, None]
    prob_target = jnp.exp(target - target_top[:, None]) / target_total[:, None]
    grad_logits = (prob_model - prob_target).astype(jnp.bfloat16)
    all_grads, late_blocks = lax.optimization_barrier(
        (gather_rows(grad_logits, dp, 7), [input_slice(i) for i in late])
    )
    for i, block in zip(late, late_blocks):
        input_blocks[i] = shifted(block, dp, per, i, 0, 0)
    half = row_count // PARTS
    products = []
    for part in range(PARTS):
        products.append(
            lax.dot_general(
                all_grads[:, part * half : (part + 1) * half].reshape(dp * half, -1),
                unembed,
                (((1,), (1,)), ((), ())),
                preferred_element_type=jnp.float32,
            ).reshape(dp, half, slice_count)
        )
    grad_cols = return_parts(products, dp, vocab)
    gain_cols = lax.dynamic_slice_in_dim(final_gain, first_col, col_count, 0)
    scaled = grad_cols * gain_cols
    inner_parts = small_gather(jnp.sum(value_cols * scaled, axis=1)[None], "vocab", vocab, 6)
    inner = jnp.sum(inner_parts, axis=0).reshape(row_count, 1) / feature_count
    grad_translated = (inv_rms * scaled - value_cols * inv_rms**3 * inner).astype(jnp.bfloat16)
    grad_translator = row_outer([input_blocks[i] for i in range(dp)], gather_rows(grad_translated, dp, 8))
    return (grad_translator, row_kl)


def whole(dp, vocab, *arrays):
    return local(dp, vocab, *arrays)


def solution(mesh):
    return jax.shard_map(
        functools.partial(whole, mesh.shape["dp"], mesh.shape["vocab"]),
        mesh=mesh,
        in_specs=(P("dp", None), P(None, "vocab"), P(), P("dp", "vocab"), P("dp", "vocab")),
        out_specs=(P("dp", "vocab"), P("dp")),
        check_vma=False,
    )
```
